32 devices in a mesh: src: 4 (over z), snk: 4 (over x, core), sub: 2 (over y).
Axes of the slice: x: 2, y: 2, z: 4, core: 2. Of those that a mesh axis runs over, the one named last changes fastest.
Arguments:
- peram: bfloat16 [4, 4, 2, 512, 512], P('src', 'snk', None, 'sub'), may hold values from -6 to 6
- elemental: bfloat16 [2, 512, 512], replicated, may hold values from -0.0078125 to 0.0078125
- spin_signs: int32 [4], replicated, may hold values from 0 to 1
- insertions: int32 [4], replicated, may hold values from 0 to 3
Outputs:
- peram_full: bfloat16 [4, 4, 2, 512, 512], P('src', 'snk', None, 'sub')
- contraction: float32 [4, 4, 2, 512, 512], P('src', 'snk', None, 'sub')
The draws below stay inside these ranges and needn't reach their ends.
Inputs may be any that keep to these rules, and one draw needn't show every extreme that they name: `spin_signs`: one entry for each of the four spin blocks. `insertions`: insertion times may repeat.
All inputs are finite; a program needn't handle non-finite values.
Results may differ from the reference program's by a relative error of at most 0.0029.
Values may be sent and summed in bfloat16 or wider, within the bound.
No kernel may reach another device: no remote copies, remote signals or barrier semaphores. Data moves between devices by JAX's collectives and lax.ppermute only.
A program may use at most 64 MiB of HBM per device.

```python
import jax
import jax.numpy as jnp
from jax import lax

NEV = 128
B = 512
NT = 4
NINS = 4


def set_ends(entries, key, least, largest):
    shape = entries.shape
    index_at = [jax.random.randint(jax.random.fold_in(key, axis), (), 0, shape[axis]) for axis in range(len(shape))]
    entries = entries.at[tuple(index_at)].set(least)
    longest = shape.index(max(shape))
    index_at[longest] = (index_at[longest] + 1) % shape[longest]
    return entries.at[tuple(index_at)].set(largest)


def steps_of(stream_key, shape, shards, low, largest):
    loudness = 1.0
    for axis_at, shards_of in shards:
        draws = jax.random.uniform(jax.random.fold_in(jax.random.fold_in(stream_key, 6), axis_at), (shards_of,), jnp.float32, low / len(shards), largest / len(shards))
        loudness = loudness * jnp.repeat(jnp.exp(draws), shape[axis_at] // shards_of).reshape((-1,) + (1,) * (len(shape) - 1 - axis_at))
    return loudness


def scatter_about(own_key, extent, deviation, bound, shards=(), held_as=jnp.bfloat16):
    array = deviation * jax.random.normal(own_key, extent, jnp.float32)
    if shards:
        array = array * steps_of(own_key, extent, shards, -0.22, 0.18)
    return jnp.clip(array, -bound, bound).astype(held_as)


def setup_inputs(seed: int = 0) -> dict:
    arg_keys = jax.random.split(jax.random.key(seed), 5)
    return {
        "peram": scatter_about(arg_keys[0], (NT, NT, 2, B, B), 1.0, 6.0, ((0, 4), (1, 4), (3, 2))),
        "elemental": scatter_about(arg_keys[1], (2, B, B), (2 * B * B) ** -0.5, 0.0078125),
        "spin_signs": set_ends(jax.random.randint(arg_keys[2], (4,), 0, 2), jax.random.fold_in(arg_keys[2], 1), 0, 1).astype(jnp.int32),
        "insertions": set_ends(jax.random.randint(arg_keys[3], (NINS,), 0, NT), jax.random.fold_in(arg_keys[3], 1), 0, NT - 1).astype(jnp.int32),
    }


def reference(peram, elemental, spin_signs, insertions):
    signs = 1.0 - 2.0 * jnp.repeat(spin_signs.astype(jnp.float32), NEV)
    flip = signs[:, None] * signs[None, :]
    swapped = jnp.swapaxes(peram, 0, 1)
    mirror_re = flip * jnp.swapaxes(swapped[:, :, 0], -1, -2).astype(jnp.float32)
    mirror_im = -flip * jnp.swapaxes(swapped[:, :, 1], -1, -2).astype(jnp.float32)
    upper = jnp.stack([mirror_re, mirror_im], axis=2).astype(jnp.bfloat16)
    row_ids = jnp.arange(NT)[:, None]
    col_ids = jnp.arange(NT)[None, :]
    lower = (row_ids >= col_ids)[:, :, None, None, None]
    full = jnp.where(lower, peram, upper)
    elem_re = elemental[0].astype(jnp.float32)
    elem_im = elemental[1].astype(jnp.float32)
    total = jnp.zeros(full.shape, jnp.float32)
    for index in range(NINS):
        moment = insertions[index].astype(jnp.int32)
        column = lax.dynamic_index_in_dim(full, moment, 1, keepdims=False).astype(jnp.float32)
        row = lax.dynamic_index_in_dim(full, moment, 0, keepdims=False).astype(jnp.float32)
        left_re = jnp.einsum('ixy,yz->ixz', column[:, 0], elem_re) - jnp.einsum('ixy,yz->ixz', column[:, 1], elem_im)
        left_im = jnp.einsum('ixy,yz->ixz', column[:, 0], elem_im) + jnp.einsum('ixy,yz->ixz', column[:, 1], elem_re)
        left = jnp.stack([left_re, left_im], axis=1).astype(jnp.bfloat16).astype(jnp.float32)

        def one_row(block):
            part_re = jnp.einsum('xy,jyz->jxz', block[0], row[:, 0]) - jnp.einsum('xy,jyz->jxz', block[1], row[:, 1])
            part_im = jnp.einsum('xy,jyz->jxz', block[0], row[:, 1]) + jnp.einsum('xy,jyz->jxz', block[1], row[:, 0])
            return jnp.stack([part_re, part_im], axis=1)

        total = total + lax.map(one_row, left)
    return full, total
```

```python
import jax
import jax.numpy as jnp
from jax import lax
from jax.sharding import PartitionSpec as P

AXES = ("src", "snk", "sub")


def complex_product(first, second):
    real_part = jnp.dot(first[0], second[0], preferred_element_type=jnp.float32) - jnp.dot(
        first[1], second[1], preferred_element_type=jnp.float32
    )
    imag_part = jnp.dot(first[0], second[1], preferred_element_type=jnp.float32) + jnp.dot(
        first[1], second[0], preferred_element_type=jnp.float32
    )
    return jnp.stack([real_part, imag_part], axis=0)


def broadcast(block, axis, owner):
    block = jnp.where(lax.axis_index(axis) == owner, block, jnp.zeros_like(block))
    return lax.psum(block, axis)


def swap(value, axis, mask):
    size = lax.axis_size(axis)
    return lax.ppermute(value, axis, [(i, i ^ mask) for i in range(size)])


def fill_upper(own, spin_signs):
    n_src, n_snk, n_sub = (lax.axis_size(axis) for axis in AXES)
    rows, width = own.shape[1:]
    half = lax.axis_index("sub")
    signs = 1.0 - 2.0 * jnp.repeat(spin_signs.astype(jnp.float32), width // spin_signs.shape[0])
    col_signs = lax.dynamic_slice_in_dim(signs, half * rows, rows)
    flip = signs[:, None] * col_signs[None, :]
    mirror_re = flip * own[0].astype(jnp.float32).T
    mirror_im = -flip * own[1].astype(jnp.float32).T
    mirrored = jnp.stack([mirror_re, mirror_im], axis=0).astype(jnp.bfloat16)
    pieces = mirrored.reshape(2, n_sub, rows, rows)

    def place(a, b, h):
        return (a * n_snk + b) * n_sub + h

    arrived = []
    for shift in range(n_sub):
        target = lax.rem(half + shift, n_sub)
        piece = lax.dynamic_index_in_dim(pieces, target, 1, keepdims=False)
        pairs = [
            (place(b, a, h), place(a, b, (h + shift) % n_sub))
            for b in range(n_src)
            for a in range(min(b, n_snk))
            if b < n_snk and a < n_src
            for h in range(n_sub)
        ]
        arrived.append(lax.ppermute(piece, AXES, pairs))
    columns = []
    for part in range(n_sub):
        column = arrived[0]
        for shift in range(1, n_sub):
            column = jnp.where(lax.rem(part + shift, n_sub) == half, arrived[shift], column)
        columns.append(column)
    upper = jnp.concatenate(columns, axis=2)
    return jnp.where(lax.axis_index("src") >= lax.axis_index("snk"), own, upper)


def by_broadcast(full_half, payload, insertions):
    n_sub = lax.axis_size("sub")
    total = jnp.zeros(full_half.shape, jnp.float32)
    for index in range(insertions.shape[0]):
        moment = insertions[index]
        received = broadcast(payload, "snk", moment)
        halves = [broadcast(full_half, ("src", "sub"), moment * n_sub + part) for part in range(n_sub)]
        total = total + complex_product(received, jnp.concatenate(halves, axis=1))
    return total


def by_doubling(full_half, payload, insertions):
    a = lax.axis_index("src")
    b = lax.axis_index("snk")
    half = lax.axis_index("sub")
    right = {0: full_half}
    right[1] = swap(full_half, "src", 1)
    right[3] = swap(full_half, "src", 3)
    left_far = swap(payload, "snk", 2)
    right[2] = swap(right[3], "src", 1)
    left_near = swap(jnp.stack([payload, left_far]), "snk", 1)
    left = jnp.stack([payload, left_near[0], left_far, left_near[1]])
    total = None
    for step in (0, 1, 3, 2):
        mine = right[step]
        other = swap(mine, "sub", 1)
        first = jnp.where(half == 0, mine, other)
        second = jnp.where(half == 0, other, mine)
        block = jnp.concatenate([first, second], axis=1)
        moment = a ^ step
        count = jnp.sum((insertions == moment).astype(jnp.float32))
        term = count * complex_product(lax.dynamic_index_in_dim(left, moment ^ b, 0, keepdims=False), block)
        total = term if total is None else total + term
    return total


def local(peram, elemental, spin_signs, insertions):
    own = peram[0, 0]
    full_half = fill_upper(own, spin_signs)
    payload = complex_product(full_half, elemental).astype(jnp.bfloat16)
    sizes = tuple(lax.axis_size(axis) for axis in AXES)
    if sizes == (4, 4, 2):
        total = by_doubling(full_half, payload, insertions)
    else:
        total = by_broadcast(full_half, payload, insertions)
    return (full_half[None, None], total[None, None])


def solution(mesh):
    return jax.shard_map(
        local,
        mesh=mesh,
        in_specs=(P("src", "snk", None, "sub", None), P(), P(), P()),
        out_specs=(P("src", "snk", None, "sub", None), P("src", "snk", None, "sub", None)),
        check_vma=False,
    )
```

```python
import jax
import jax.numpy as jnp
from jax import lax
from jax.experimental import pallas as pl
from jax.experimental.pallas import tpu as pltpu
from jax.sharding import PartitionSpec as P

AXES = ("src", "snk", "sub")


def complex_product(first, second):
    real_part = jnp.dot(first[0], second[0], preferred_element_type=jnp.float32) - jnp.dot(
        first[1], second[1], preferred_element_type=jnp.float32
    )
    imag_part = jnp.dot(first[0], second[1], preferred_element_type=jnp.float32) + jnp.dot(
        first[1], second[0], preferred_element_type=jnp.float32
    )
    return jnp.stack([real_part, imag_part], axis=0)


def broadcast(block, axis, owner):
    block = jnp.where(lax.axis_index(axis) == owner, block, jnp.zeros_like(block))
    return lax.psum(block, axis)


def swap(value, axis, mask):
    size = lax.axis_size(axis)
    return lax.ppermute(value, axis, [(i, i ^ mask) for i in range(size)])


def scalars(*values):
    return jnp.stack([jnp.asarray(value, jnp.int32) for value in values])


SMEM = pl.BlockSpec(memory_space=pltpu.SMEM)
VMEM = pl.BlockSpec(memory_space=pltpu.VMEM)


def local_call(kernel, out_shape, operands, tables=2, scratch=(), flops=0):
    outs = out_shape if isinstance(out_shape, (list, tuple)) else [out_shape]
    moved = sum(x.size * x.dtype.itemsize for x in (*operands, *outs))
    return pl.pallas_call(
        kernel,
        out_shape=out_shape,
        in_specs=[SMEM] * tables + [VMEM] * (len(operands) - tables),
        out_specs=jax.tree.map(lambda _: VMEM, out_shape),
        scratch_shapes=scratch,
        cost_estimate=pl.CostEstimate(flops=flops, bytes_accessed=moved, transcendentals=0),
    )(*operands)


def mirror_kernel(place_ref, sign_ref, own_ref, *out_refs):
    half = place_ref[0]
    rows, width = own_ref.shape[1:]
    group = width // sign_ref.shape[0]
    n_sub = len(out_refs)
    for shift in range(n_sub):
        target = lax.rem(half + shift, n_sub)
        start = target * rows
        for i in range(0, rows, group):
            for j in range(0, rows, group):
                row = sign_ref[(target * rows + i) // group]
                column = sign_ref[(half * rows + j) // group]
                flip = ((1 - 2 * row) * (1 - 2 * column)).astype(jnp.float32)
                for part, scale in ((0, flip), (1, -flip)):
                    block = own_ref[part, j : j + group, pl.ds(pl.multiple_of(start + i, 128), group)]
                    block = scale * block.astype(jnp.float32).T
                    out_refs[shift][part, i : i + group, j : j + group] = block.astype(jnp.bfloat16)


def mirror_pieces(own, spin_signs):
    n_sub = lax.axis_size("sub")
    rows = own.shape[1]
    piece = jax.ShapeDtypeStruct((2, rows, rows), own.dtype)
    return local_call(mirror_kernel, [piece] * n_sub, (scalars(lax.axis_index("sub")), spin_signs, own))


def place(a, b, h):
    return (a * lax.axis_size("snk") + b) * lax.axis_size("sub") + h


def send(value, pairs):
    return lax.ppermute(value, AXES, pairs)


def mirror_pairs(shift, chosen):
    n_src, n_snk, n_sub = (lax.axis_size(axis) for axis in AXES)
    return [
        (place(b, a, h), place(a, b, (h + shift) % n_sub))
        for b in range(min(n_src, n_snk))
        for a in range(b)
        if chosen(b, a)
        for h in range(n_sub)
    ]


def assemble(own, arrived):
    n_sub = lax.axis_size("sub")
    half = lax.axis_index("sub")
    columns = []
    for part in range(n_sub):
        column = arrived[0]
        for shift in range(1, n_sub):
            column = jnp.where(lax.rem(part + shift, n_sub) == half, arrived[shift], column)
        columns.append(column)
    upper = jnp.concatenate(columns, axis=2)
    return jnp.where(lax.axis_index("src") >= lax.axis_index("snk"), own, upper)


def fill_upper(own, spin_signs):
    pieces = mirror_pieces(own, spin_signs)
    shifts = range(lax.axis_size("sub"))
    return assemble(own, [send(pieces[k], mirror_pairs(k, lambda b, a: True)) for k in shifts])


def by_broadcast(full_half, payload, insertions):
    n_sub = lax.axis_size("sub")
    total = jnp.zeros(full_half.shape, jnp.float32)
    for index in range(insertions.shape[0]):
        moment = insertions[index]
        received = broadcast(payload, "snk", moment)
        halves = [broadcast(full_half, ("src", "sub"), moment * n_sub + part) for part in range(n_sub)]
        total = total + complex_product(received, jnp.concatenate(halves, axis=1))
    return total


def left_panel(keep, give):
    n_snk, n_sub = lax.axis_size("snk"), lax.axis_size("sub")
    across = [(b * n_sub + h, (b ^ 2) * n_sub + (h ^ 1)) for b in range(n_snk) for h in range(n_sub)]
    give_y = swap(give, "sub", 1)
    keep_x = swap(keep, "snk", 2)
    give_x = lax.ppermute(give, ("snk", "sub"), across)
    near = jnp.concatenate([keep, give_y], axis=1)
    far = jnp.concatenate([keep_x, give_x], axis=1)
    near_other = swap(near, "snk", 1)
    far_other = swap(far, "snk", 1)
    return near, near_other, far, far_other


def dot(first, second):
    return jnp.dot(first, second, preferred_element_type=jnp.float32)


def home_kernel(table, _, own, direct0, direct1, hand0, hand1, elem, home, home0, home1, keep, give):
    lower, relayed, half = table[0], table[1], table[2]
    rows = own.shape[1]

    @pl.when(lower == 1)
    def _():
        home[...] = own[...]

    def put(first, second):
        home[:, :, pl.ds(pl.multiple_of(half * rows, 128), rows)] = first[...]
        home[:, :, pl.ds(pl.multiple_of((1 - half) * rows, 128), rows)] = second[...]

    @pl.when((lower == 0) & (relayed == 0))
    def _():
        put(direct0, direct1)

    @pl.when((lower == 0) & (relayed == 1))
    def _():
        put(hand0, hand1)

    home0[...] = home[:, :, :rows]
    home1[...] = home[:, :, rows:]
    for start, out in ((half, keep), (1 - half, give)):
        columns = pl.ds(pl.multiple_of(start * rows, 128), rows)
        out[0] = (dot(home[0], elem[0, :, columns]) - dot(home[1], elem[1, :, columns])).astype(jnp.bfloat16)
        out[1] = (dot(home[0], elem[1, :, columns]) + dot(home[1], elem[0, :, columns])).astype(jnp.bfloat16)


def pick_kernel(table, _, early, late0, late1, out0, out1):
    rows = out0.shape[2]

    @pl.when(table[0] == 1)
    def _():
        out0[...] = early[:, :, :rows]
        out1[...] = early[:, :, rows:]

    @pl.when(table[0] == 0)
    def _():
        out0[...] = late0[...]
        out1[...] = late1[...]


def times(ins, moment):
    count = jnp.int32(0)
    for index in range(ins.shape[0]):
        count = count + (ins[index] == moment).astype(jnp.int32)
    return count.astype(jnp.float32)


def product(count, left, right):
    real = count * (dot(left[0], right[0]) - dot(left[1], right[1]))
    imag = count * (dot(left[0], right[1]) + dot(left[1], right[0]))
    return real, imag


def early_kernel(table, ins, left0, left1, left2, left3, home0, home1, near_early, near, far0, far1, acc, last, chosen, beside):
    a, b, near_ready = table[0], table[1], table[2]
    rows = home0.shape[2]

    def choose(k, out):
        for index, left in enumerate((left0, left1, left2, left3)):

            @pl.when(k == index)
            def _():
                out[...] = left[...]

    @pl.when(near_ready == 1)
    def _():
        beside[...] = near_early[...]

    @pl.when(near_ready == 0)
    def _():
        beside[...] = near[...]

    for step in (0, 1, 3):
        choose(a ^ step ^ b, chosen)
        count = times(ins, a ^ step)
        for part in range(2):
            columns = slice(part * rows, (part + 1) * rows)
            right = {0: (home0, home1)[part], 1: beside.at[:, :, columns], 3: (far0, far1)[part]}[step]
            real, imag = product(count, chosen, right)
            if step:
                real = acc[0, :, columns] + real
                imag = acc[1, :, columns] + imag
            acc[0, :, columns] = real
            acc[1, :, columns] = imag
    choose(a ^ 2 ^ b, last)


def late_kernel(part, table, ins, acc, last, block, mine, give):
    rows = mine.shape[1]
    columns = slice(part * rows, (part + 1) * rows)
    real, imag = product(times(ins, table[0] ^ 2), last, block)
    for index, value in ((0, real), (1, imag)):
        total = acc[index, :, columns] + value
        mine[index] = total[:rows]
        give[index] = total[rows:].astype(jnp.bfloat16)


def finish_kernel(table, _, mine0, given0, mine1, given1, out):
    rows = mine0.shape[1]
    out[:, :, :rows] = mine0[...] + given0[...].astype(jnp.float32)
    out[:, :, rows:] = mine1[...] + given1[...].astype(jnp.float32)


def along_z(mask, chosen):
    return [
        (place(a, b, h), place(a ^ mask, b, h))
        for a in range(lax.axis_size("src"))
        for b in range(lax.axis_size("snk"))
        if chosen(a, b)
        for h in range(lax.axis_size("sub"))
    ]


def by_doubling(own, elemental, spin_signs, insertions):
    a = lax.axis_index("src")
    b = lax.axis_index("snk")
    rows, width = own.shape[1:]
    parts = range(width // rows)
    shifts = range(lax.axis_size("sub"))

    def relayed(b, a):
        return (b, a) == (3, 1)

    def ready(a, b):
        return a >= b

    def ready_far(a, b):
        return a >= b and (b >= 2 or a < 2)

    pieces = mirror_pieces(own, spin_signs)
    relay = [send(pieces[k], [(place(3, 1, h), place(3, 3, (h + k) % 2)) for h in shifts]) for k in shifts]
    direct = [send(pieces[k], mirror_pairs(k, lambda b, a: not relayed(b, a))) for k in shifts]
    handed = [send(relay[k], [(place(3, 3, h), place(1, 3, h)) for h in shifts]) for k in shifts]
    near_early = send(own, along_z(1, ready))
    far_early = send(own, along_z(3, ready_far))

    piece = jax.ShapeDtypeStruct((2, rows, rows), own.dtype)
    tile = jax.ShapeDtypeStruct(own.shape, own.dtype)
    full_half, home0, home1, keep, give = local_call(
        home_kernel,
        [tile, piece, piece, piece, piece],
        (scalars(a >= b, (a == 1) & (b == 3), lax.axis_index("sub")), spin_signs, own, *direct, *handed, elemental),
        flops=8 * rows * width * width,
    )
    far_late = [send(value, along_z(3, lambda a, b: not ready_far(a, b))) for value in (home0, home1)]
    near = send(full_half, along_z(1, lambda a, b: not ready(a, b)))
    from_far = a ^ 3
    was_ready = (from_far >= b) & ((b >= 2) | (from_far < 2))
    far = local_call(pick_kernel, [piece, piece], (scalars(was_ready), spin_signs, far_early, *far_late))
    late = [swap(far[part], "src", 1) for part in parts]
    left = left_panel(keep, give)
    table = scalars(a, b, (a ^ 1) >= b)
    acc, last = local_call(
        early_kernel,
        [jax.ShapeDtypeStruct((2, 2 * rows, width), jnp.float32), jax.ShapeDtypeStruct((2, 2 * rows, rows), own.dtype)],
        (table, insertions, *left, home0, home1, near_early, near, *far),
        scratch=[pltpu.VMEM((2, 2 * rows, rows), own.dtype), pltpu.VMEM(own.shape, own.dtype)],
        flops=3 * 16 * rows * rows * width,
    )
    ends = []
    for part in parts:
        mine, given = local_call(
            lambda *refs, part=part: late_kernel(part, *refs),
            [jax.ShapeDtypeStruct((2, rows, rows), jnp.float32), piece],
            (table, insertions, acc, last, late[part]),
            flops=16 * rows * rows * rows,
        )
        ends += [mine, swap(given, "sub", 1)]
    total = local_call(finish_kernel, jax.ShapeDtypeStruct(own.shape, jnp.float32), (table, insertions, *ends))
    return full_half, total


def local(peram, elemental, spin_signs, insertions):
    own = peram[0, 0]
    if lax.axis_size("src") == lax.axis_size("snk") == 4 and lax.axis_size("sub") == 2:
        full_half, total = by_doubling(own, elemental, spin_signs, insertions)
    else:
        full_half = fill_upper(own, spin_signs)
        payload = complex_product(full_half, elemental).astype(jnp.bfloat16)
        total = by_broadcast(full_half, payload, insertions)
    return (full_half[None, None], total[None, None])


def solution(mesh):
    return jax.shard_map(
        local,
        mesh=mesh,
        in_specs=(P("src", "snk", None, "sub", None), P(), P(), P()),
        out_specs=(P("src", "snk", None, "sub", None), P("src", "snk", None, "sub", None)),
        check_vma=False,
    )
```

```python
import jax
import jax.numpy as jnp
from jax import lax
from jax.experimental import pallas as pl
from jax.experimental.pallas import tpu as pltpu
from jax.sharding import PartitionSpec as P

AXES = ("src", "snk", "sub")


def complex_product(first, second):
    real_part = jnp.dot(first[0], second[0], preferred_element_type=jnp.float32) - jnp.dot(
        first[1], second[1], preferred_element_type=jnp.float32
    )
    imag_part = jnp.dot(first[0], second[1], preferred_element_type=jnp.float32) + jnp.dot(
        first[1], second[0], preferred_element_type=jnp.float32
    )
    return jnp.stack([real_part, imag_part], axis=0)


def broadcast(block, axis, owner):
    block = jnp.where(lax.axis_index(axis) == owner, block, jnp.zeros_like(block))
    return lax.psum(block, axis)


def swap(value, axis, mask):
    size = lax.axis_size(axis)
    return lax.ppermute(value, axis, [(i, i ^ mask) for i in range(size)])


SMEM = pl.BlockSpec(memory_space=pltpu.SMEM)
VMEM = pl.BlockSpec(memory_space=pltpu.VMEM)


def local_call(kernel, out_shape, operands, tables=0, scratch=(), flops=0, limit=16 * 2**20):
    outs = out_shape if isinstance(out_shape, (list, tuple)) else [out_shape]
    moved = sum(x.size * x.dtype.itemsize for x in (*operands, *outs))
    return pl.pallas_call(
        kernel,
        out_shape=out_shape,
        in_specs=[SMEM] * tables + [VMEM] * (len(operands) - tables),
        out_specs=jax.tree.map(lambda _: VMEM, out_shape),
        scratch_shapes=scratch,
        cost_estimate=pl.CostEstimate(flops=flops, bytes_accessed=moved, transcendentals=0),
        compiler_params=pltpu.CompilerParams(vmem_limit_bytes=limit),
    )(*operands)


def mirror_kernel(sign_ref, own_ref, *out_refs):
    half = lax.axis_index("sub")
    rows, width = own_ref.shape[1:]
    group = width // sign_ref.shape[0]
    *out_refs, copy_ref = out_refs
    copy_ref[...] = own_ref[...]
    n_sub = len(out_refs)
    for shift in range(n_sub):
        target = lax.rem(half + shift, n_sub)
        start = target * rows
        for i in range(0, rows, group):
            for j in range(0, rows, group):
                row = sign_ref[(target * rows + i) // group]
                column = sign_ref[(half * rows + j) // group]
                flip = ((1 - 2 * row) * (1 - 2 * column)).astype(jnp.float32)
                for part, scale in ((0, flip), (1, -flip)):
                    block = own_ref[part, j : j + group, pl.ds(pl.multiple_of(start + i, 128), group)]
                    block = scale * block.astype(jnp.float32).T
                    out_refs[shift][part, i : i + group, j : j + group] = block.astype(jnp.bfloat16)


def mirror_pieces(own, spin_signs):
    n_sub = lax.axis_size("sub")
    rows = own.shape[1]
    piece = jax.ShapeDtypeStruct((2, rows, rows), own.dtype)
    whole = jax.ShapeDtypeStruct(own.shape, own.dtype)
    *pieces, own = local_call(mirror_kernel, [piece] * n_sub + [whole], (spin_signs, own), tables=1)
    return pieces, own


def place(a, b, h):
    return (a * lax.axis_size("snk") + b) * lax.axis_size("sub") + h


def send(value, pairs):
    return lax.ppermute(value, AXES, pairs)


def mirror_pairs(shift, chosen):
    n_src, n_snk, n_sub = (lax.axis_size(axis) for axis in AXES)
    return [
        (place(b, a, h), place(a, b, (h + shift) % n_sub))
        for b in range(min(n_src, n_snk))
        for a in range(b)
        if chosen(b, a)
        for h in range(n_sub)
    ]


def assemble(own, arrived):
    n_sub = lax.axis_size("sub")
    half = lax.axis_index("sub")
    columns = []
    for part in range(n_sub):
        column = arrived[0]
        for shift in range(1, n_sub):
            column = jnp.where(lax.rem(part + shift, n_sub) == half, arrived[shift], column)
        columns.append(column)
    upper = jnp.concatenate(columns, axis=2)
    return jnp.where(lax.axis_index("src") >= lax.axis_index("snk"), own, upper)


def fill_upper(own, spin_signs):
    pieces, own = mirror_pieces(own, spin_signs)
    shifts = range(lax.axis_size("sub"))
    return assemble(own, [send(pieces[k], mirror_pairs(k, lambda b, a: True)) for k in shifts])


def by_broadcast(full_half, payload, insertions):
    n_sub = lax.axis_size("sub")
    total = jnp.zeros(full_half.shape, jnp.float32)
    for index in range(insertions.shape[0]):
        moment = insertions[index]
        received = broadcast(payload, "snk", moment)
        halves = [broadcast(full_half, ("src", "sub"), moment * n_sub + part) for part in range(n_sub)]
        total = total + complex_product(received, jnp.concatenate(halves, axis=1))
    return total


def left_panel(keep, give):
    n_snk, n_sub = lax.axis_size("snk"), lax.axis_size("sub")
    across = [(b * n_sub + h, (b ^ 2) * n_sub + (h ^ 1)) for b in range(n_snk) for h in range(n_sub)]
    give_y = swap(give, "sub", 1)
    keep_x = swap(keep, "snk", 2)
    give_x = lax.ppermute(give, ("snk", "sub"), across)
    near = jnp.concatenate([keep, give_y], axis=1)
    far = jnp.concatenate([keep_x, give_x], axis=1)
    near_other = swap(near, "snk", 1)
    far_other = swap(far, "snk", 1)
    return near, near_other, far, far_other


def dot(first, second):
    return jnp.dot(first, second, preferred_element_type=jnp.float32)


def stage_kernel(value, out):
    out[...] = value[...]


def home_kernel(own, direct0, direct1, hand0, hand1, elem, home, home0, home1, keep, give):
    a, b, half = (lax.axis_index(axis) for axis in AXES)
    lower = a >= b
    relayed = (a == 1) & (b == 3)
    rows = own.shape[1]

    @pl.when(lower)
    def _():
        home[...] = own[...]

    def put(first, second):
        home[:, :, pl.ds(pl.multiple_of(half * rows, 128), rows)] = first[...]
        home[:, :, pl.ds(pl.multiple_of((1 - half) * rows, 128), rows)] = second[...]

    @pl.when(jnp.logical_not(lower | relayed))
    def _():
        put(direct0, direct1)

    @pl.when(relayed)
    def _():
        put(hand0, hand1)

    home0[...] = home[:, :, :rows]
    home1[...] = home[:, :, rows:]
    for start, out in ((half, keep), (1 - half, give)):
        columns = pl.ds(pl.multiple_of(start * rows, 128), rows)
        out[0] = (dot(home[0], elem[0, :, columns]) - dot(home[1], elem[1, :, columns])).astype(jnp.bfloat16)
        out[1] = (dot(home[0], elem[1, :, columns]) + dot(home[1], elem[0, :, columns])).astype(jnp.bfloat16)


def ready(a, b):
    return a >= b


def ready_far(a, b):
    return (a >= b) & ((b >= 2) | (a < 2))


def pick_kernel(part, early, late, out):
    rows = out.shape[2]
    was_ready = ready_far(lax.axis_index("src") ^ 3, lax.axis_index("snk"))

    @pl.when(was_ready)
    def _():
        out[...] = early[:, :, part * rows : (part + 1) * rows]

    @pl.when(jnp.logical_not(was_ready))
    def _():
        out[...] = late[...]


def times(ins, moment):
    count = jnp.int32(0)
    for index in range(ins.shape[0]):
        count = count + (ins[index] == moment).astype(jnp.int32)
    return count.astype(jnp.float32)


def product(count, left, right):
    real = count * (dot(left[0], right[0]) - dot(left[1], right[1]))
    imag = count * (dot(left[0], right[1]) + dot(left[1], right[0]))
    return real, imag


def early_kernel(ins, left0, left1, left2, left3, home0, home1, near_early, near, far0, far1, acc, last, chosen, beside):
    a, b = lax.axis_index("src"), lax.axis_index("snk")
    near_ready = ready(a ^ 1, b)
    rows = home0.shape[2]

    def choose(k, out):
        for index, left in enumerate((left0, left1, left2, left3)):

            @pl.when(k == index)
            def _():
                out[...] = left[...]

    @pl.when(near_ready)
    def _():
        beside[...] = near_early[...]

    @pl.when(jnp.logical_not(near_ready))
    def _():
        beside[...] = near[...]

    for step in (0, 1, 3):
        choose(a ^ step ^ b, chosen)
        count = times(ins, a ^ step)
        for part in range(2):
            columns = slice(part * rows, (part + 1) * rows)
            right = {0: (home0, home1)[part], 1: beside.at[:, :, columns], 3: (far0, far1)[part]}[step]
            real, imag = product(count, chosen, right)
            if step:
                real = acc[0, :, columns] + real
                imag = acc[1, :, columns] + imag
            acc[0, :, columns] = real
            acc[1, :, columns] = imag
    choose(a ^ 2 ^ b, last)


def late_kernel(part, ins, acc, last, block, mine, give):
    rows = mine.shape[1]
    columns = slice(part * rows, (part + 1) * rows)
    real, imag = product(times(ins, lax.axis_index("src") ^ 2), last, block)
    for index, value in ((0, real), (1, imag)):
        total = acc[index, :, columns] + value
        mine[index] = total[:rows]
        give[index] = total[rows:].astype(jnp.bfloat16)


def finish_kernel(mine0, given0, mine1, given1, out):
    rows = mine0.shape[1]
    out[:, :, :rows] = mine0[...] + given0[...].astype(jnp.float32)
    out[:, :, rows:] = mine1[...] + given1[...].astype(jnp.float32)


def along_z(mask, chosen):
    return [
        (place(a, b, h), place(a ^ mask, b, h))
        for a in range(lax.axis_size("src"))
        for b in range(lax.axis_size("snk"))
        if chosen(a, b)
        for h in range(lax.axis_size("sub"))
    ]


def by_doubling(own, elemental, spin_signs, insertions):
    rows, width = own.shape[1:]
    parts = range(width // rows)
    shifts = range(lax.axis_size("sub"))

    def relayed(b, a):
        return (b, a) == (3, 1)

    pieces, own = mirror_pieces(own, spin_signs)
    relay = [send(pieces[k], [(place(3, 1, h), place(3, 3, (h + k) % 2)) for h in shifts]) for k in shifts]
    direct = [send(pieces[k], mirror_pairs(k, lambda b, a: not relayed(b, a))) for k in shifts]
    handed = [send(relay[k], [(place(3, 3, h), place(1, 3, h)) for h in shifts]) for k in shifts]
    elemental = local_call(stage_kernel, jax.ShapeDtypeStruct(elemental.shape, elemental.dtype), (elemental,))
    own, elemental = lax.optimization_barrier((own, elemental))
    near_early = send(own, along_z(1, ready))
    far_early = send(own, along_z(3, ready_far))

    piece = jax.ShapeDtypeStruct((2, rows, rows), own.dtype)
    tile = jax.ShapeDtypeStruct(own.shape, own.dtype)
    full_half, home0, home1, keep, give = local_call(
        home_kernel,
        [tile, piece, piece, piece, piece],
        (own, *direct, *handed, elemental),
        flops=8 * rows * width * width,
    )
    far_late = [send(value, along_z(3, lambda a, b: not ready_far(a, b))) for value in (home0, home1)]
    near = send(full_half, along_z(1, lambda a, b: not ready(a, b)))
    far = [
        local_call(lambda *refs, part=part: pick_kernel(part, *refs), piece, (far_early, far_late[part]))
        for part in parts
    ]
    late = [swap(far[part], "src", 1) for part in parts]
    left = left_panel(keep, give)
    acc, last = local_call(
        early_kernel,
        [jax.ShapeDtypeStruct((2, 2 * rows, width), jnp.float32), jax.ShapeDtypeStruct((2, 2 * rows, rows), own.dtype)],
        (insertions, *left, home0, home1, near_early, near, *far),
        tables=1,
        scratch=[pltpu.VMEM((2, 2 * rows, rows), own.dtype), pltpu.VMEM(own.shape, own.dtype)],
        flops=3 * 16 * rows * rows * width,
    )
    ends = []
    for part in parts:
        mine, given = local_call(
            lambda *refs, part=part: late_kernel(part, *refs),
            [jax.ShapeDtypeStruct((2, rows, rows), jnp.float32), piece],
            (insertions, acc, last, late[part]),
            tables=1,
            flops=16 * rows * rows * rows,
        )
        ends += [mine, swap(given, "sub", 1)]
    total = local_call(finish_kernel, jax.ShapeDtypeStruct(own.shape, jnp.float32), tuple(ends))
    return full_half, total


def local(peram, elemental, spin_signs, insertions):
    own = peram[0, 0]
    if lax.axis_size("src") == lax.axis_size("snk") == 4 and lax.axis_size("sub") == 2:
        full_half, total = by_doubling(own, elemental, spin_signs, insertions)
    else:
        full_half = fill_upper(own, spin_signs)
        payload = complex_product(full_half, elemental).astype(jnp.bfloat16)
        total = by_broadcast(full_half, payload, insertions)
    return (full_half[None, None], total[None, None])


def solution(mesh):
    return jax.shard_map(
        local,
        mesh=mesh,
        in_specs=(P("src", "snk", None, "sub", None), P(), P(), P()),
        out_specs=(P("src", "snk", None, "sub", None), P("src", "snk", None, "sub", None)),
        check_vma=False,
    )
```

```python
import jax
import jax.numpy as jnp
from jax import lax
from jax.experimental import pallas as pl
from jax.experimental.pallas import tpu as pltpu
from jax.sharding import PartitionSpec as P

AXES = ("src", "snk", "sub")


def complex_product(first, second):
    real_part = jnp.dot(first[0], second[0], preferred_element_type=jnp.float32) - jnp.dot(
        first[1], second[1], preferred_element_type=jnp.float32
    )
    imag_part = jnp.dot(first[0], second[1], preferred_element_type=jnp.float32) + jnp.dot(
        first[1], second[0], preferred_element_type=jnp.float32
    )
    return jnp.stack([real_part, imag_part], axis=0)


def broadcast(block, axis, owner):
    block = jnp.where(lax.axis_index(axis) == owner, block, jnp.zeros_like(block))
    return lax.psum(block, axis)


def swap(value, axis, mask):
    size = lax.axis_size(axis)
    return lax.ppermute(value, axis, [(i, i ^ mask) for i in range(size)])


SMEM = pl.BlockSpec(memory_space=pltpu.SMEM)
VMEM = pl.BlockSpec(memory_space=pltpu.VMEM)


def local_call(kernel, out_shape, operands, tables=0, scratch=(), flops=0, limit=16 * 2**20):
    outs = out_shape if isinstance(out_shape, (list, tuple)) else [out_shape]
    moved = sum(x.size * x.dtype.itemsize for x in (*operands, *outs))
    return pl.pallas_call(
        kernel,
        out_shape=out_shape,
        in_specs=[SMEM] * tables + [VMEM] * (len(operands) - tables),
        out_specs=jax.tree.map(lambda _: VMEM, out_shape),
        scratch_shapes=scratch,
        cost_estimate=pl.CostEstimate(flops=flops, bytes_accessed=moved, transcendentals=0),
        compiler_params=pltpu.CompilerParams(vmem_limit_bytes=limit),
    )(*operands)


def mirror_kernel(sign_ref, own_ref, *out_refs):
    half = lax.axis_index("sub")
    rows, width = own_ref.shape[1:]
    group = width // sign_ref.shape[0]
    *out_refs, copy_ref = out_refs
    copy_ref[...] = own_ref[...]
    n_sub = len(out_refs)
    for shift in range(n_sub):
        target = lax.rem(half + shift, n_sub)
        start = target * rows
        for i in range(0, rows, group):
            for j in range(0, rows, group):
                row = sign_ref[(target * rows + i) // group]
                column = sign_ref[(half * rows + j) // group]
                flip = ((1 - 2 * row) * (1 - 2 * column)).astype(jnp.float32)
                for part, scale in ((0, flip), (1, -flip)):
                    block = own_ref[part, j : j + group, pl.ds(pl.multiple_of(start + i, 128), group)]
                    block = scale * block.astype(jnp.float32).T
                    out_refs[shift][part, i : i + group, j : j + group] = block.astype(jnp.bfloat16)


def mirror_pieces(own, spin_signs):
    n_sub = lax.axis_size("sub")
    rows = own.shape[1]
    piece = jax.ShapeDtypeStruct((2, rows, rows), own.dtype)
    whole = jax.ShapeDtypeStruct(own.shape, own.dtype)
    *pieces, own = local_call(mirror_kernel, [piece] * n_sub + [whole], (spin_signs, own), tables=1)
    return pieces, own


def place(a, b, h):
    return (a * lax.axis_size("snk") + b) * lax.axis_size("sub") + h


def send(value, pairs):
    return lax.ppermute(value, AXES, pairs)


def mirror_pairs(shift, chosen):
    n_src, n_snk, n_sub = (lax.axis_size(axis) for axis in AXES)
    return [
        (place(b, a, h), place(a, b, (h + shift) % n_sub))
        for b in range(min(n_src, n_snk))
        for a in range(b)
        if chosen(b, a)
        for h in range(n_sub)
    ]


def assemble(own, arrived):
    n_sub = lax.axis_size("sub")
    half = lax.axis_index("sub")
    columns = []
    for part in range(n_sub):
        column = arrived[0]
        for shift in range(1, n_sub):
            column = jnp.where(lax.rem(part + shift, n_sub) == half, arrived[shift], column)
        columns.append(column)
    upper = jnp.concatenate(columns, axis=2)
    return jnp.where(lax.axis_index("src") >= lax.axis_index("snk"), own, upper)


def fill_upper(own, spin_signs):
    pieces, own = mirror_pieces(own, spin_signs)
    shifts = range(lax.axis_size("sub"))
    return assemble(own, [send(pieces[k], mirror_pairs(k, lambda b, a: True)) for k in shifts])


def by_broadcast(full_half, payload, insertions):
    n_sub = lax.axis_size("sub")
    total = jnp.zeros(full_half.shape, jnp.float32)
    for index in range(insertions.shape[0]):
        moment = insertions[index]
        received = broadcast(payload, "snk", moment)
        halves = [broadcast(full_half, ("src", "sub"), moment * n_sub + part) for part in range(n_sub)]
        total = total + complex_product(received, jnp.concatenate(halves, axis=1))
    return total


def left_panel(keep, give):
    n_snk, n_sub = lax.axis_size("snk"), lax.axis_size("sub")
    across = [(b * n_sub + h, (b ^ 2) * n_sub + (h ^ 1)) for b in range(n_snk) for h in range(n_sub)]
    give_y = swap(give, "sub", 1)
    keep_x = swap(keep, "snk", 2)
    give_x = lax.ppermute(give, ("snk", "sub"), across)
    near = jnp.concatenate([keep, give_y], axis=1)
    far = jnp.concatenate([keep_x, give_x], axis=1)
    near_other = swap(near, "snk", 1)
    far_other = swap(far, "snk", 1)
    return near, near_other, far, far_other


def dot(first, second):
    return jnp.dot(first, second, preferred_element_type=jnp.float32)


def stage_kernel(value, out):
    out[...] = value[...]


def home_kernel(own, direct0, direct1, hand0, hand1, elem, home, home0, home1, keep, give):
    a, b, half = (lax.axis_index(axis) for axis in AXES)
    lower = a >= b
    relayed = (a == 0) & (b == 3)
    rows = own.shape[1]

    @pl.when(lower)
    def _():
        home[...] = own[...]

    def put(first, second):
        home[:, :, pl.ds(pl.multiple_of(half * rows, 128), rows)] = first[...]
        home[:, :, pl.ds(pl.multiple_of((1 - half) * rows, 128), rows)] = second[...]

    @pl.when(jnp.logical_not(lower | relayed))
    def _():
        put(direct0, direct1)

    @pl.when(relayed)
    def _():
        put(hand0, hand1)

    home0[...] = home[:, :, :rows]
    home1[...] = home[:, :, rows:]
    for start, out in ((half, keep), (1 - half, give)):
        columns = pl.ds(pl.multiple_of(start * rows, 128), rows)
        out[0] = (dot(home[0], elem[0, :, columns]) - dot(home[1], elem[1, :, columns])).astype(jnp.bfloat16)
        out[1] = (dot(home[0], elem[1, :, columns]) + dot(home[1], elem[0, :, columns])).astype(jnp.bfloat16)


def ready(a, b):
    return a >= b


def ready_far(a, b):
    return (a >= b) & ((b >= 2) | (a < 2))


def pick(was_ready, early, late, out):
    @pl.when(was_ready)
    def _():
        out[...] = early[...]

    @pl.when(jnp.logical_not(was_ready))
    def _():
        out[...] = late[...]


def times(ins, moment):
    count = jnp.int32(0)
    for index in range(ins.shape[0]):
        count = count + (ins[index] == moment).astype(jnp.int32)
    return count.astype(jnp.float32)


def product(count, left, right):
    real = count * (dot(left[0], right[0]) - dot(left[1], right[1]))
    imag = count * (dot(left[0], right[1]) + dot(left[1], right[0]))
    return real, imag


def choose(lefts, step, out):
    k = lax.axis_index("src") ^ lax.axis_index("snk") ^ step
    for index, left in enumerate(lefts):

        @pl.when(k == index)
        def _():
            out[...] = left[...]


def early_kernel(
    ins, left0, left1, left2, left3, home0, home1, far_early, far0, far1, acc, left_near, left_last, chosen, block
):
    a, b = lax.axis_index("src"), lax.axis_index("snk")
    lefts = (left0, left1, left2, left3)
    rows = home0.shape[2]
    for step in (0, 3):
        choose(lefts, step, chosen)
        count = times(ins, a ^ step)
        for part in range(2):
            columns = slice(part * rows, (part + 1) * rows)
            if step == 0:
                acc[0, :, columns], acc[1, :, columns] = product(count, chosen, (home0, home1)[part])
            else:
                pick(ready_far(a ^ 3, b), far_early.at[:, :, columns], (far0, far1)[part], block)
                real, imag = product(count, chosen, block)
                acc[0, :, columns] += real
                acc[1, :, columns] += imag
    choose(lefts, 1, left_near)
    choose(lefts, 2, left_last)


def late_kernel(part, ins, acc, left_near, left_last, near_early, near, skip, late, mine, give, block):
    rows = mine.shape[1]
    columns = slice(part * rows, (part + 1) * rows)
    a, b = lax.axis_index("src"), lax.axis_index("snk")
    pick(ready(a ^ 1, b), near_early.at[:, :, columns], near.at[:, :, columns], block)
    first = product(times(ins, a ^ 1), left_near, block)
    pick(ready_far(a ^ 2, b), skip.at[:, :, columns], late, block)
    second = product(times(ins, a ^ 2), left_last, block)
    for index in range(2):
        total = acc[index, :, columns] + first[index] + second[index]
        mine[index] = total[:rows]
        give[index] = total[rows:].astype(jnp.bfloat16)


def finish_kernel(mine0, given0, mine1, given1, out):
    rows = mine0.shape[1]
    out[:, :, :rows] = mine0[...] + given0[...].astype(jnp.float32)
    out[:, :, rows:] = mine1[...] + given1[...].astype(jnp.float32)


def along_z(mask, chosen):
    return [
        (place(a, b, h), place(a ^ mask, b, h))
        for a in range(lax.axis_size("src"))
        for b in range(lax.axis_size("snk"))
        if chosen(a, b)
        for h in range(lax.axis_size("sub"))
    ]


def by_doubling(own, elemental, spin_signs, insertions):
    rows, width = own.shape[1:]
    parts = range(width // rows)
    shifts = range(lax.axis_size("sub"))

    def relayed(b, a):
        return (b, a) == (3, 0)

    pieces, own = mirror_pieces(own, spin_signs)
    relay = [send(pieces[k], [(place(3, 0, h), place(3, 2, (h + k) % 2)) for h in shifts]) for k in shifts]
    direct = [send(pieces[k], mirror_pairs(k, lambda b, a: not relayed(b, a))) for k in shifts]
    handed = [send(relay[k], [(place(3, 2, h), place(0, 3, h)) for h in shifts]) for k in shifts]
    elemental = local_call(stage_kernel, jax.ShapeDtypeStruct(elemental.shape, elemental.dtype), (elemental,))
    own, elemental = lax.optimization_barrier((own, elemental))
    skip_early = send(own, along_z(2, ready_far))
    far_early = send(own, along_z(3, ready_far))
    near_early = send(own, along_z(1, ready))

    piece = jax.ShapeDtypeStruct((2, rows, rows), own.dtype)
    tile = jax.ShapeDtypeStruct(own.shape, own.dtype)
    full_half, home0, home1, keep, give = local_call(
        home_kernel,
        [tile, piece, piece, piece, piece],
        (own, *direct, *handed, elemental),
        flops=8 * rows * width * width,
    )
    far_late = [send(value, along_z(3, lambda a, b: not ready_far(a, b))) for value in (home0, home1)]
    near = send(full_half, along_z(1, lambda a, b: not ready(a, b)))
    late = [send(far_late[part], along_z(1, lambda a, b: not ready_far(a ^ 3, b))) for part in parts]
    left = left_panel(keep, give)
    panel = jax.ShapeDtypeStruct((2, 2 * rows, rows), own.dtype)
    acc, *lefts = local_call(
        early_kernel,
        [jax.ShapeDtypeStruct((2, 2 * rows, width), jnp.float32), panel, panel],
        (insertions, *left, home0, home1, far_early, *far_late),
        tables=1,
        scratch=[pltpu.VMEM(panel.shape, panel.dtype), pltpu.VMEM(piece.shape, piece.dtype)],
        flops=2 * 16 * rows * rows * width,
    )
    ends = []
    for part in parts:
        mine, given = local_call(
            lambda *refs, part=part: late_kernel(part, *refs),
            [jax.ShapeDtypeStruct((2, rows, rows), jnp.float32), piece],
            (insertions, acc, *lefts, near_early, near, skip_early, late[part]),
            tables=1,
            scratch=[pltpu.VMEM((2, rows, rows), own.dtype)],
            flops=16 * rows * rows * rows,
        )
        ends += [mine, swap(given, "sub", 1)]
    total = local_call(finish_kernel, jax.ShapeDtypeStruct(own.shape, jnp.float32), tuple(ends))
    return full_half, total


def local(peram, elemental, spin_signs, insertions):
    own = peram[0, 0]
    if lax.axis_size("src") == lax.axis_size("snk") == 4 and lax.axis_size("sub") == 2:
        full_half, total = by_doubling(own, elemental, spin_signs, insertions)
    else:
        full_half = fill_upper(own, spin_signs)
        payload = complex_product(full_half, elemental).astype(jnp.bfloat16)
        total = by_broadcast(full_half, payload, insertions)
    return (full_half[None, None], total[None, None])


def solution(mesh):
    return jax.shard_map(
        local,
        mesh=mesh,
        in_specs=(P("src", "snk", None, "sub", None), P(), P(), P()),
        out_specs=(P("src", "snk", None, "sub", None), P("src", "snk", None, "sub", None)),
        check_vma=False,
    )
```

```python
import jax
import jax.numpy as jnp
from jax import lax
from jax.experimental import pallas as pl
from jax.experimental.pallas import tpu as pltpu
from jax.sharding import PartitionSpec as P

AXES = ("src", "snk", "sub")


def complex_product(first, second):
    real_part = jnp.dot(first[0], second[0], preferred_element_type=jnp.float32) - jnp.dot(
        first[1], second[1], preferred_element_type=jnp.float32
    )
    imag_part = jnp.dot(first[0], second[1], preferred_element_type=jnp.float32) + jnp.dot(
        first[1], second[0], preferred_element_type=jnp.float32
    )
    return jnp.stack([real_part, imag_part], axis=0)


def broadcast(block, axis, owner):
    block = jnp.where(lax.axis_index(axis) == owner, block, jnp.zeros_like(block))
    return lax.psum(block, axis)


def swap(value, axis, mask):
    size = lax.axis_size(axis)
    return lax.ppermute(value, axis, [(i, i ^ mask) for i in range(size)])


SMEM = pl.BlockSpec(memory_space=pltpu.SMEM)
VMEM = pl.BlockSpec(memory_space=pltpu.VMEM)


def local_call(kernel, out_shape, operands, tables=0, scratch=(), flops=0, limit=16 * 2**20):
    outs = out_shape if isinstance(out_shape, (list, tuple)) else [out_shape]
    moved = sum(x.size * x.dtype.itemsize for x in (*operands, *outs))
    return pl.pallas_call(
        kernel,
        out_shape=out_shape,
        in_specs=[SMEM] * tables + [VMEM] * (len(operands) - tables),
        out_specs=jax.tree.map(lambda _: VMEM, out_shape),
        scratch_shapes=scratch,
        cost_estimate=pl.CostEstimate(flops=flops, bytes_accessed=moved, transcendentals=0),
        compiler_params=pltpu.CompilerParams(vmem_limit_bytes=limit),
    )(*operands)


def mirror_kernel(sign_ref, own_ref, *out_refs):
    half = lax.axis_index("sub")
    rows, width = own_ref.shape[1:]
    group = width // sign_ref.shape[0]
    *out_refs, copy_ref = out_refs
    copy_ref[...] = own_ref[...]
    n_sub = len(out_refs)
    for shift in range(n_sub):
        target = lax.rem(half + shift, n_sub)
        start = target * rows
        for i in range(0, rows, group):
            for j in range(0, rows, group):
                row = sign_ref[(target * rows + i) // group]
                column = sign_ref[(half * rows + j) // group]
                flip = ((1 - 2 * row) * (1 - 2 * column)).astype(jnp.float32)
                for part, scale in ((0, flip), (1, -flip)):
                    block = own_ref[part, j : j + group, pl.ds(pl.multiple_of(start + i, 128), group)]
                    block = scale * block.astype(jnp.float32).T
                    out_refs[shift][part, i : i + group, j : j + group] = block.astype(jnp.bfloat16)


def mirror_pieces(own, spin_signs):
    n_sub = lax.axis_size("sub")
    rows = own.shape[1]
    piece = jax.ShapeDtypeStruct((2, rows, rows), own.dtype)
    whole = jax.ShapeDtypeStruct(own.shape, own.dtype)
    *pieces, own = local_call(mirror_kernel, [piece] * n_sub + [whole], (spin_signs, own), tables=1)
    return pieces, own


def place(a, b, h):
    return (a * lax.axis_size("snk") + b) * lax.axis_size("sub") + h


def send(value, pairs):
    return lax.ppermute(value, AXES, pairs)


def mirror_pairs(shift, chosen):
    n_src, n_snk, n_sub = (lax.axis_size(axis) for axis in AXES)
    return [
        (place(b, a, h), place(a, b, (h + shift) % n_sub))
        for b in range(min(n_src, n_snk))
        for a in range(b)
        if chosen(b, a)
        for h in range(n_sub)
    ]


def assemble(own, arrived):
    n_sub = lax.axis_size("sub")
    half = lax.axis_index("sub")
    columns = []
    for part in range(n_sub):
        column = arrived[0]
        for shift in range(1, n_sub):
            column = jnp.where(lax.rem(part + shift, n_sub) == half, arrived[shift], column)
        columns.append(column)
    upper = jnp.concatenate(columns, axis=2)
    return jnp.where(lax.axis_index("src") >= lax.axis_index("snk"), own, upper)


def fill_upper(own, spin_signs):
    pieces, own = mirror_pieces(own, spin_signs)
    shifts = range(lax.axis_size("sub"))
    return assemble(own, [send(pieces[k], mirror_pairs(k, lambda b, a: True)) for k in shifts])


def by_broadcast(full_half, payload, insertions):
    n_sub = lax.axis_size("sub")
    total = jnp.zeros(full_half.shape, jnp.float32)
    for index in range(insertions.shape[0]):
        moment = insertions[index]
        received = broadcast(payload, "snk", moment)
        halves = [broadcast(full_half, ("src", "sub"), moment * n_sub + part) for part in range(n_sub)]
        total = total + complex_product(received, jnp.concatenate(halves, axis=1))
    return total


def left_panel(keep, give):
    n_snk, n_sub = lax.axis_size("snk"), lax.axis_size("sub")
    across = [(b * n_sub + h, (b ^ 2) * n_sub + (h ^ 1)) for b in range(n_snk) for h in range(n_sub)]
    give_y = swap(give, "sub", 1)
    keep_x = swap(keep, "snk", 2)
    give_x = lax.ppermute(give, ("snk", "sub"), across)
    near = jnp.concatenate([keep, give_y], axis=1)
    far = jnp.concatenate([keep_x, give_x], axis=1)
    near_other = swap(near, "snk", 1)
    far_other = swap(far, "snk", 1)
    return near, near_other, far, far_other


def dot(first, second):
    return jnp.dot(first, second, preferred_element_type=jnp.float32)


def stage_kernel(value, out):
    out[...] = value[...]


def home_kernel(own, direct0, direct1, hand0, hand1, elem, home, home0, home1, keep, give):
    a, b, half = (lax.axis_index(axis) for axis in AXES)
    lower = a >= b
    relayed = (a == 0) & (b == 3)
    rows = own.shape[1]

    @pl.when(lower)
    def _():
        home[...] = own[...]

    def put(first, second):
        home[:, :, pl.ds(pl.multiple_of(half * rows, 128), rows)] = first[...]
        home[:, :, pl.ds(pl.multiple_of((1 - half) * rows, 128), rows)] = second[...]

    @pl.when(jnp.logical_not(lower | relayed))
    def _():
        put(direct0, direct1)

    @pl.when(relayed)
    def _():
        put(hand0, hand1)

    home0[...] = home[:, :, :rows]
    home1[...] = home[:, :, rows:]
    for start, out in ((half, keep), (1 - half, give)):
        columns = pl.ds(pl.multiple_of(start * rows, 128), rows)
        out[0] = (dot(home[0], elem[0, :, columns]) - dot(home[1], elem[1, :, columns])).astype(jnp.bfloat16)
        out[1] = (dot(home[0], elem[1, :, columns]) + dot(home[1], elem[0, :, columns])).astype(jnp.bfloat16)


def ready(a, b):
    return a >= b


def ready_far(a, b):
    return (a >= b) & ((b >= 2) | (a == 1))


def pick(was_ready, early, late, out):
    @pl.when(was_ready)
    def _():
        out[...] = early[...]

    @pl.when(jnp.logical_not(was_ready))
    def _():
        out[...] = late[...]


def times(ins, moment):
    count = jnp.int32(0)
    for index in range(ins.shape[0]):
        count = count + (ins[index] == moment).astype(jnp.int32)
    return count.astype(jnp.float32)


def product(count, left, right):
    real = count * (dot(left[0], right[0]) - dot(left[1], right[1]))
    imag = count * (dot(left[0], right[1]) + dot(left[1], right[0]))
    return real, imag


def choose(lefts, step, out):
    k = lax.axis_index("src") ^ lax.axis_index("snk") ^ step
    for index, left in enumerate(lefts):

        @pl.when(k == index)
        def _():
            out[...] = left[...]


def early_kernel(
    ins, left0, left1, left2, left3, home0, home1, far_early, far0, far1, acc, left_near, left_last, chosen, block
):
    a, b = lax.axis_index("src"), lax.axis_index("snk")
    lefts = (left0, left1, left2, left3)
    rows = home0.shape[2]
    for step in (0, 3):
        choose(lefts, step, chosen)
        count = times(ins, a ^ step)
        for part in range(2):
            columns = slice(part * rows, (part + 1) * rows)
            if step == 0:
                acc[0, :, columns], acc[1, :, columns] = product(count, chosen, (home0, home1)[part])
            else:
                pick(ready_far(a ^ 3, b), far_early.at[:, :, columns], (far0, far1)[part], block)
                real, imag = product(count, chosen, block)
                acc[0, :, columns] += real
                acc[1, :, columns] += imag
    choose(lefts, 1, left_near)
    choose(lefts, 2, left_last)


def late_kernel(part, ins, acc, left_near, left_last, near_early, near, skip, hop, late, mine, give, block):
    rows = mine.shape[1]
    columns = slice(part * rows, (part + 1) * rows)
    a, b = lax.axis_index("src"), lax.axis_index("snk")
    pick(ready(a ^ 1, b), near_early.at[:, :, columns], near.at[:, :, columns], block)
    first = product(times(ins, a ^ 1), left_near, block)
    hopped = (a == 1) & (b >= 2)
    pick(ready_far(a ^ 2, b) & jnp.logical_not(hopped), skip.at[:, :, columns], late, block)

    @pl.when(hopped)
    def _():
        block[...] = hop[:, :, columns]

    second = product(times(ins, a ^ 2), left_last, block)
    for index in range(2):
        total = acc[index, :, columns] + first[index] + second[index]
        mine[index] = total[:rows]
        give[index] = total[rows:].astype(jnp.bfloat16)


def finish_kernel(mine0, given0, mine1, given1, out):
    rows = mine0.shape[1]
    out[:, :, :rows] = mine0[...] + given0[...].astype(jnp.float32)
    out[:, :, rows:] = mine1[...] + given1[...].astype(jnp.float32)


def along_z(mask, chosen):
    return [
        (place(a, b, h), place(a ^ mask, b, h))
        for a in range(lax.axis_size("src"))
        for b in range(lax.axis_size("snk"))
        if chosen(a, b)
        for h in range(lax.axis_size("sub"))
    ]


def by_doubling(own, elemental, spin_signs, insertions):
    rows, width = own.shape[1:]
    parts = range(width // rows)
    shifts = range(lax.axis_size("sub"))

    def relayed(b, a):
        return (b, a) == (3, 0)

    pieces, own = mirror_pieces(own, spin_signs)
    relay = [send(pieces[k], [(place(3, 0, h), place(3, 2, (h + k) % 2)) for h in shifts]) for k in shifts]
    direct = [send(pieces[k], mirror_pairs(k, lambda b, a: not relayed(b, a))) for k in shifts]
    handed = [send(relay[k], [(place(3, 2, h), place(0, 3, h)) for h in shifts]) for k in shifts]
    elemental = local_call(stage_kernel, jax.ShapeDtypeStruct(elemental.shape, elemental.dtype), (elemental,))
    own, elemental = lax.optimization_barrier((own, elemental))
    skip_early = send(own, along_z(2, lambda a, b: ready_far(a, b) and a < 3))
    far_early = send(own, along_z(3, ready_far))
    near_early = send(own, along_z(1, ready))

    piece = jax.ShapeDtypeStruct((2, rows, rows), own.dtype)
    tile = jax.ShapeDtypeStruct(own.shape, own.dtype)
    full_half, home0, home1, keep, give = local_call(
        home_kernel,
        [tile, piece, piece, piece, piece],
        (own, *direct, *handed, elemental),
        flops=8 * rows * width * width,
    )
    hop = send(near_early, [(place(2, b, h), place(1, b, h)) for b in range(2, 4) for h in shifts])
    far_late = [send(value, along_z(3, lambda a, b: not ready_far(a, b))) for value in (home0, home1)]
    near = send(full_half, along_z(1, lambda a, b: not ready(a, b)))
    late = [send(far_late[part], along_z(1, lambda a, b: not ready_far(a ^ 3, b))) for part in parts]
    left = left_panel(keep, give)
    panel = jax.ShapeDtypeStruct((2, 2 * rows, rows), own.dtype)
    acc, *lefts = local_call(
        early_kernel,
        [jax.ShapeDtypeStruct((2, 2 * rows, width), jnp.float32), panel, panel],
        (insertions, *left, home0, home1, far_early, *far_late),
        tables=1,
        scratch=[pltpu.VMEM(panel.shape, panel.dtype), pltpu.VMEM(piece.shape, piece.dtype)],
        flops=2 * 16 * rows * rows * width,
    )
    ends = []
    for part in parts:
        mine, given = local_call(
            lambda *refs, part=part: late_kernel(part, *refs),
            [jax.ShapeDtypeStruct((2, rows, rows), jnp.float32), piece],
            (insertions, acc, *lefts, near_early, near, skip_early, hop, late[part]),
            tables=1,
            scratch=[pltpu.VMEM((2, rows, rows), own.dtype)],
            flops=16 * rows * rows * rows,
        )
        ends += [mine, swap(given, "sub", 1)]
    total = local_call(finish_kernel, jax.ShapeDtypeStruct(own.shape, jnp.float32), tuple(ends))
    return full_half, total


def local(peram, elemental, spin_signs, insertions):
    own = peram[0, 0]
    if lax.axis_size("src") == lax.axis_size("snk") == 4 and lax.axis_size("sub") == 2:
        full_half, total = by_doubling(own, elemental, spin_signs, insertions)
    else:
        full_half = fill_upper(own, spin_signs)
        payload = complex_product(full_half, elemental).astype(jnp.bfloat16)
        total = by_broadcast(full_half, payload, insertions)
    return (full_half[None, None], total[None, None])


def solution(mesh):
    return jax.shard_map(
        local,
        mesh=mesh,
        in_specs=(P("src", "snk", None, "sub", None), P(), P(), P()),
        out_specs=(P("src", "snk", None, "sub", None), P("src", "snk", None, "sub", None)),
        check_vma=False,
    )
```

```python
import jax
import jax.numpy as jnp
from jax import lax
from jax.experimental import pallas as pl
from jax.experimental.pallas import tpu as pltpu
from jax.sharding import PartitionSpec as P

AXES = ("src", "snk", "sub")


def complex_product(first, second):
    real_part = jnp.dot(first[0], second[0], preferred_element_type=jnp.float32) - jnp.dot(
        first[1], second[1], preferred_element_type=jnp.float32
    )
    imag_part = jnp.dot(first[0], second[1], preferred_element_type=jnp.float32) + jnp.dot(
        first[1], second[0], preferred_element_type=jnp.float32
    )
    return jnp.stack([real_part, imag_part], axis=0)


def broadcast(block, axis, owner):
    block = jnp.where(lax.axis_index(axis) == owner, block, jnp.zeros_like(block))
    return lax.psum(block, axis)


def swap(value, axis, mask):
    size = lax.axis_size(axis)
    return lax.ppermute(value, axis, [(i, i ^ mask) for i in range(size)])


SMEM = pl.BlockSpec(memory_space=pltpu.SMEM)
VMEM = pl.BlockSpec(memory_space=pltpu.VMEM)


def local_call(kernel, out_shape, operands, tables=0, scratch=(), flops=0, limit=16 * 2**20):
    outs = out_shape if isinstance(out_shape, (list, tuple)) else [out_shape]
    moved = sum(x.size * x.dtype.itemsize for x in (*operands, *outs))
    return pl.pallas_call(
        kernel,
        out_shape=out_shape,
        in_specs=[SMEM] * tables + [VMEM] * (len(operands) - tables),
        out_specs=jax.tree.map(lambda _: VMEM, out_shape),
        scratch_shapes=scratch,
        cost_estimate=pl.CostEstimate(flops=flops, bytes_accessed=moved, transcendentals=0),
        compiler_params=pltpu.CompilerParams(vmem_limit_bytes=limit),
    )(*operands)


def mirror_kernel(sign_ref, own_ref, *out_refs):
    half = lax.axis_index("sub")
    rows, width = own_ref.shape[1:]
    group = width // sign_ref.shape[0]
    *out_refs, copy_ref = out_refs
    copy_ref[...] = own_ref[...]
    n_sub = len(out_refs)
    for shift in range(n_sub):
        target = lax.rem(half + shift, n_sub)
        start = target * rows
        for i in range(0, rows, group):
            for j in range(0, rows, group):
                row = sign_ref[(target * rows + i) // group]
                column = sign_ref[(half * rows + j) // group]
                flip = ((1 - 2 * row) * (1 - 2 * column)).astype(jnp.float32)
                for part, scale in ((0, flip), (1, -flip)):
                    block = own_ref[part, j : j + group, pl.ds(pl.multiple_of(start + i, 128), group)]
                    block = scale * block.astype(jnp.float32).T
                    out_refs[shift][part, i : i + group, j : j + group] = block.astype(jnp.bfloat16)


def mirror_pieces(own, spin_signs):
    n_sub = lax.axis_size("sub")
    rows = own.shape[1]
    piece = jax.ShapeDtypeStruct((2, rows, rows), own.dtype)
    whole = jax.ShapeDtypeStruct(own.shape, own.dtype)
    *pieces, own = local_call(mirror_kernel, [piece] * n_sub + [whole], (spin_signs, own), tables=1)
    return pieces, own


def place(a, b, h):
    return (a * lax.axis_size("snk") + b) * lax.axis_size("sub") + h


def send(value, pairs):
    return lax.ppermute(value, AXES, pairs)


def mirror_pairs(shift, chosen):
    n_src, n_snk, n_sub = (lax.axis_size(axis) for axis in AXES)
    return [
        (place(b, a, h), place(a, b, (h + shift) % n_sub))
        for b in range(min(n_src, n_snk))
        for a in range(b)
        if chosen(b, a)
        for h in range(n_sub)
    ]


def assemble(own, arrived):
    n_sub = lax.axis_size("sub")
    half = lax.axis_index("sub")
    columns = []
    for part in range(n_sub):
        column = arrived[0]
        for shift in range(1, n_sub):
            column = jnp.where(lax.rem(part + shift, n_sub) == half, arrived[shift], column)
        columns.append(column)
    upper = jnp.concatenate(columns, axis=2)
    return jnp.where(lax.axis_index("src") >= lax.axis_index("snk"), own, upper)


def fill_upper(own, spin_signs):
    pieces, own = mirror_pieces(own, spin_signs)
    shifts = range(lax.axis_size("sub"))
    return assemble(own, [send(pieces[k], mirror_pairs(k, lambda b, a: True)) for k in shifts])


def by_broadcast(full_half, payload, insertions):
    n_sub = lax.axis_size("sub")
    total = jnp.zeros(full_half.shape, jnp.float32)
    for index in range(insertions.shape[0]):
        moment = insertions[index]
        received = broadcast(payload, "snk", moment)
        halves = [broadcast(full_half, ("src", "sub"), moment * n_sub + part) for part in range(n_sub)]
        total = total + complex_product(received, jnp.concatenate(halves, axis=1))
    return total


def left_panel(keep, give):
    n_snk, n_sub = lax.axis_size("snk"), lax.axis_size("sub")
    across = [(b * n_sub + h, (b ^ 2) * n_sub + (h ^ 1)) for b in range(n_snk) for h in range(n_sub)]
    give_y = swap(give, "sub", 1)
    keep_x = swap(keep, "snk", 2)
    give_x = lax.ppermute(give, ("snk", "sub"), across)
    near = jnp.concatenate([keep, give_y], axis=1)
    far = jnp.concatenate([keep_x, give_x], axis=1)
    near_other = swap(near, "snk", 1)
    far_other = swap(far, "snk", 1)
    return near, near_other, far, far_other


def dot(first, second):
    return jnp.dot(first, second, preferred_element_type=jnp.float32)


def stage_kernel(value, out):
    out[...] = value[...]


def home_kernel(own, direct0, direct1, hand0, hand1, elem, home, home0, home1, keep, give):
    a, b, half = (lax.axis_index(axis) for axis in AXES)
    lower = a >= b
    relayed = (a == 0) & (b == 3)
    rows = own.shape[1]

    @pl.when(lower)
    def _():
        home[...] = own[...]

    def put(first, second):
        home[:, :, pl.ds(pl.multiple_of(half * rows, 128), rows)] = first[...]
        home[:, :, pl.ds(pl.multiple_of((1 - half) * rows, 128), rows)] = second[...]

    @pl.when(jnp.logical_not(lower | relayed))
    def _():
        put(direct0, direct1)

    @pl.when(relayed)
    def _():
        put(hand0, hand1)

    home0[...] = home[:, :, :rows]
    home1[...] = home[:, :, rows:]
    for start, out in ((half, keep), (1 - half, give)):
        columns = pl.ds(pl.multiple_of(start * rows, 128), rows)
        out[0] = (dot(home[0], elem[0, :, columns]) - dot(home[1], elem[1, :, columns])).astype(jnp.bfloat16)
        out[1] = (dot(home[0], elem[1, :, columns]) + dot(home[1], elem[0, :, columns])).astype(jnp.bfloat16)


def ready(a, b):
    return a >= b


def ready_far(a, b):
    return (a >= b) & ((b >= 2) | (a == 1))


def pick(was_ready, early, late, out):
    @pl.when(was_ready)
    def _():
        out[...] = early[...]

    @pl.when(jnp.logical_not(was_ready))
    def _():
        out[...] = late[...]


def times(ins, moment):
    count = jnp.int32(0)
    for index in range(ins.shape[0]):
        count = count + (ins[index] == moment).astype(jnp.int32)
    return count.astype(jnp.float32)


def product(count, left, right):
    real = count * (dot(left[0], right[0]) - dot(left[1], right[1]))
    imag = count * (dot(left[0], right[1]) + dot(left[1], right[0]))
    return real, imag


def choose(lefts, step, out):
    k = lax.axis_index("src") ^ lax.axis_index("snk") ^ step
    for index, left in enumerate(lefts):

        @pl.when(k == index)
        def _():
            out[...] = left[...]


def early_kernel(
    ins, left0, left1, left2, left3, home0, home1, far_early, far0, far1, acc, left_near, left_last, chosen, block
):
    a, b = lax.axis_index("src"), lax.axis_index("snk")
    lefts = (left0, left1, left2, left3)
    rows = home0.shape[2]
    for step in (0, 3):
        choose(lefts, step, chosen)
        count = times(ins, a ^ step)
        for part in range(2):
            columns = slice(part * rows, (part + 1) * rows)
            if step == 0:
                acc[0, :, columns], acc[1, :, columns] = product(count, chosen, (home0, home1)[part])
            else:
                pick(ready_far(a ^ 3, b), far_early.at[:, :, columns], (far0, far1)[part], block)
                real, imag = product(count, chosen, block)
                acc[0, :, columns] += real
                acc[1, :, columns] += imag
    choose(lefts, 1, left_near)
    choose(lefts, 2, left_last)


def late_kernel(part, ins, acc, left_near, left_last, near_early, near, skip, hop, late, mine, give, block):
    rows = mine.shape[1]
    columns = slice(part * rows, (part + 1) * rows)
    a, b = lax.axis_index("src"), lax.axis_index("snk")
    pick(ready(a ^ 1, b), near_early.at[:, :, columns], near.at[:, :, columns], block)
    first = product(times(ins, a ^ 1), left_near, block)
    hopped = (a == 1) & (b >= 2)
    pick(ready_far(a ^ 2, b) & jnp.logical_not(hopped), skip.at[:, :, columns], late, block)

    @pl.when(hopped)
    def _():
        block[...] = hop[:, :, columns]

    second = product(times(ins, a ^ 2), left_last, block)
    for index in range(2):
        total = acc[index, :, columns] + first[index] + second[index]
        mine[index] = total[:rows]
        give[index] = total[rows:].astype(jnp.bfloat16)


def finish_kernel(part, mine, given, *refs):
    out, total, sem = refs[-3:]
    rows = mine.shape[1]
    total[...] = mine[...] + given[...].astype(jnp.float32)
    copy = pltpu.make_async_copy(total, out.at[:, :, part * rows : (part + 1) * rows], sem)
    copy.start()
    copy.wait()


def finish(part, mine, given, width, *whole):
    anywhere = pl.BlockSpec(memory_space=pltpu.HBM)
    return pl.pallas_call(
        lambda *refs: finish_kernel(part, *refs),
        out_shape=jax.ShapeDtypeStruct((*mine.shape[:2], width), jnp.float32),
        in_specs=[VMEM, VMEM] + [anywhere] * len(whole),
        out_specs=anywhere,
        scratch_shapes=[pltpu.VMEM(mine.shape, jnp.float32), pltpu.SemaphoreType.DMA],
        input_output_aliases={2: 0} if whole else {},
        compiler_params=pltpu.CompilerParams(vmem_limit_bytes=16 * 2**20),
    )(mine, given, *whole)


def along_z(mask, chosen):
    return [
        (place(a, b, h), place(a ^ mask, b, h))
        for a in range(lax.axis_size("src"))
        for b in range(lax.axis_size("snk"))
        if chosen(a, b)
        for h in range(lax.axis_size("sub"))
    ]


def by_doubling(own, elemental, spin_signs, insertions):
    rows, width = own.shape[1:]
    parts = range(width // rows)
    shifts = range(lax.axis_size("sub"))

    def relayed(b, a):
        return (b, a) == (3, 0)

    pieces, own = mirror_pieces(own, spin_signs)
    relay = [send(pieces[k], [(place(3, 0, h), place(3, 2, (h + k) % 2)) for h in shifts]) for k in shifts]
    direct = [send(pieces[k], mirror_pairs(k, lambda b, a: not relayed(b, a))) for k in shifts]
    handed = [send(relay[k], [(place(3, 2, h), place(0, 3, h)) for h in shifts]) for k in shifts]
    elemental = local_call(stage_kernel, jax.ShapeDtypeStruct(elemental.shape, elemental.dtype), (elemental,))
    own, elemental = lax.optimization_barrier((own, elemental))
    skip_early = send(own, along_z(2, lambda a, b: ready_far(a, b) and a < 3))
    far_early = send(own, along_z(3, ready_far))
    near_early = send(own, along_z(1, ready))

    piece = jax.ShapeDtypeStruct((2, rows, rows), own.dtype)
    tile = jax.ShapeDtypeStruct(own.shape, own.dtype)
    full_half, home0, home1, keep, give = local_call(
        home_kernel,
        [tile, piece, piece, piece, piece],
        (own, *direct, *handed, elemental),
        flops=8 * rows * width * width,
    )
    hop = send(near_early, [(place(2, b, h), place(1, b, h)) for b in range(2, 4) for h in shifts])
    far_late = [send(value, along_z(3, lambda a, b: not ready_far(a, b))) for value in (home0, home1)]
    near = send(full_half, along_z(1, lambda a, b: not ready(a, b)))
    late = [send(far_late[part], along_z(1, lambda a, b: not ready_far(a ^ 3, b))) for part in parts]
    left = left_panel(keep, give)
    panel = jax.ShapeDtypeStruct((2, 2 * rows, rows), own.dtype)
    acc, *lefts = local_call(
        early_kernel,
        [jax.ShapeDtypeStruct((2, 2 * rows, width), jnp.float32), panel, panel],
        (insertions, *left, home0, home1, far_early, *far_late),
        tables=1,
        scratch=[pltpu.VMEM(panel.shape, panel.dtype), pltpu.VMEM(piece.shape, piece.dtype)],
        flops=2 * 16 * rows * rows * width,
    )
    ends = []
    for part in parts:
        mine, given = local_call(
            lambda *refs, part=part: late_kernel(part, *refs),
            [jax.ShapeDtypeStruct((2, rows, rows), jnp.float32), piece],
            (insertions, acc, *lefts, near_early, near, skip_early, hop, late[part]),
            tables=1,
            scratch=[pltpu.VMEM((2, rows, rows), own.dtype)],
            flops=16 * rows * rows * rows,
        )
        ends += [mine, swap(given, "sub", 1)]
    total = finish(0, *ends[:2], width)
    total = finish(1, *ends[2:], width, total)
    return full_half, total


def local(peram, elemental, spin_signs, insertions):
    own = peram[0, 0]
    if lax.axis_size("src") == lax.axis_size("snk") == 4 and lax.axis_size("sub") == 2:
        full_half, total = by_doubling(own, elemental, spin_signs, insertions)
    else:
        full_half = fill_upper(own, spin_signs)
        payload = complex_product(full_half, elemental).astype(jnp.bfloat16)
        total = by_broadcast(full_half, payload, insertions)
    return (full_half[None, None], total[None, None])


def solution(mesh):
    return jax.shard_map(
        local,
        mesh=mesh,
        in_specs=(P("src", "snk", None, "sub", None), P(), P(), P()),
        out_specs=(P("src", "snk", None, "sub", None), P("src", "snk", None, "sub", None)),
        check_vma=False,
    )
```
